32 devices in a mesh: sec: 4 (over y, core), row: 8 (over z, x).
Axes of the slice: x: 2, y: 2, z: 4, core: 2. Of those that a mesh axis runs over, the one named last changes fastest.
Arguments:
- section_image: float32 [4, 128, 2048], P('sec', 'row'), may hold values from -6 to 6
- drift_offsets: int32 [4, 2], replicated, may hold values from -4 to 4, as said below
- stem_weight: float32 [28, 1, 5, 5], replicated, may hold values from -1.25 to 1.25
- stem_bias: float32 [28], replicated, may hold values from -3 to 3
- first_weight: bfloat16 [28, 28, 3, 3, 3], replicated, may hold values from -0.21875 to 0.21875
- first_bias: float32 [28], replicated, may hold values from -3 to 3
- second_weight: bfloat16 [28, 28, 3, 3, 3], replicated, may hold values from -0.21875 to 0.21875
- second_bias: float32 [28], replicated, may hold values from -3 to 3
Outputs:
- volume_out: bfloat16 [28, 4, 64, 1024], P(None, None, 'row', 'sec')
The draws below stay inside these ranges and needn't reach their ends.
Inputs may be any that keep to these rules, and one draw needn't show every extreme that they name: `drift_offsets`: offsets lie within plus or minus 4.
All inputs are finite; a program needn't handle non-finite values.
Results may differ from the reference program's by a relative error of at most 0.0049.
Values may be sent and summed in bfloat16 or wider, within the bound.
A program may use at most 64 MiB of HBM per device.

```python
import jax
import jax.numpy as jnp
from jax import lax

C = 28
MAXD = 4
W = 2048
SECTIONS = 4
ROWS = 128
OW = 1024
CW = 256
N_SEC = 4


def draw_drift_offsets(key, part):
    base = jax.random.randint(jax.random.fold_in(key, 11), (SECTIONS, 2), -MAXD, MAXD + 1)
    picks = jax.random.randint(jax.random.fold_in(key, 12), (2,), 0, SECTIONS)
    base = base.at[picks[0], 0].set(MAXD)
    base = base.at[picks[1], 1].set(-MAXD)
    return base.astype(jnp.int32)


def levels(rng, dims, shards, low, high):
    level, own = 1.0, jax.random.fold_in(rng, 6)
    for position, shards_of in shards:
        steps = jnp.exp(jax.random.uniform(jax.random.fold_in(own, position), (shards_of,), jnp.float32, low / len(shards), high / len(shards)))
        level = level * jnp.repeat(steps, dims[position] // shards_of).reshape([-1 if axis == position else 1 for axis in range(len(dims))])
    return level


def bell_draw(own_key, shape, width, reach, cuts=(), kind=jnp.bfloat16):
    values = width * jax.random.normal(own_key, shape, jnp.float32)
    if cuts:
        values = values * levels(own_key, shape, cuts, -0.22, 0.18)
    return jnp.clip(values, -reach, reach).astype(kind)


def setup_inputs(seed: int = 0) -> dict:
    key_of = jax.random.split(jax.random.key(seed), 9)
    return {
        "section_image": bell_draw(key_of[0], (SECTIONS, ROWS, W), 1.0, 6.0, ((0, 4), (1, 8)), jnp.float32),
        "drift_offsets": draw_drift_offsets(jax.random.fold_in(key_of[8], 71), 0),
        "stem_weight": bell_draw(key_of[2], (C, 1, 5, 5), 25 ** -0.5, 1.25, (), jnp.float32),
        "stem_bias": bell_draw(key_of[3], (C,), 0.5, 3.0, (), jnp.float32),
        "first_weight": bell_draw(key_of[4], (C, C, 3, 3, 3), (27 * C) ** -0.5, 0.21875),
        "first_bias": bell_draw(key_of[5], (C,), 0.5, 3.0, (), jnp.float32),
        "second_weight": bell_draw(key_of[6], (C, C, 3, 3, 3), (27 * C) ** -0.5, 0.21875),
        "second_bias": bell_draw(key_of[7], (C,), 0.5, 3.0, (), jnp.float32),
    }


def stem_layer(section_image, stem_weight, stem_bias):
    def stem_one(section):
        result = lax.conv_general_dilated(section[None, None], stem_weight, (2, 2), ((2, 1), (2, 1)), dimension_numbers=("NCHW", "OIHW", "NCHW"), precision=lax.Precision.HIGHEST)
        return jax.nn.relu(result[0] + stem_bias[:, None, None]).astype(jnp.bfloat16)
    features = lax.map(stem_one, section_image)
    return jnp.transpose(features, (1, 0, 2, 3))


def align_sections(features, drift_offsets):
    padded = jnp.pad(features, ((0, 0), (0, 0), (MAXD, MAXD), (MAXD, MAXD)))
    out_rows = features.shape[2]
    out_cols = features.shape[3]

    def select_window(one_block, offsets):
        return lax.dynamic_slice(one_block, (jnp.int32(0), (offsets[0] + MAXD).astype(jnp.int32), (offsets[1] + MAXD).astype(jnp.int32)), (one_block.shape[0], out_rows, out_cols))
    return jax.vmap(select_window, in_axes=(1, 0), out_axes=1)(padded, drift_offsets)


def volume_conv(padded_field, weight):
    result = lax.conv_general_dilated(padded_field[None], weight, (1, 1, 1), ((1, 1), (0, 0), (0, 0)), dimension_numbers=("NCDHW", "OIDHW", "NCDHW"), preferred_element_type=jnp.float32)
    return result[0]


def reference(section_image, drift_offsets, stem_weight, stem_bias, first_weight, first_bias, second_weight, second_bias):
    aligned = align_sections(stem_layer(section_image, stem_weight, stem_bias), drift_offsets)
    out_rows = aligned.shape[2]
    padded = jnp.pad(aligned, ((0, 0), (0, 0), (2, 2), (2, 2)))

    def one_block(block_index):
        first_col = (block_index * CW).astype(jnp.int32)
        window = lax.dynamic_slice_in_dim(padded, first_col, CW + 4, 3)
        hidden = volume_conv(window, first_weight) + first_bias[:, None, None, None]
        row_pos = jnp.arange(out_rows + 2) - 1
        col_pos = jnp.arange(CW + 2) - 1 + first_col
        in_image = ((row_pos >= 0) & (row_pos < out_rows))[:, None] & ((col_pos >= 0) & (col_pos < OW))[None, :]
        hidden = jnp.where(in_image, jax.nn.relu(hidden), jnp.float32(0.0)).astype(jnp.bfloat16)
        combined = volume_conv(hidden, second_weight) + second_bias[:, None, None, None] + window[:, :, 2:-2, 2:-2].astype(jnp.float32)
        return combined.astype(jnp.bfloat16)
    blocks = lax.map(one_block, jnp.arange(N_SEC, dtype=jnp.int32))
    return jnp.moveaxis(blocks, 0, 3).reshape(aligned.shape[0], SECTIONS, out_rows, OW)
```

```python
import functools

import jax
import jax.numpy as jnp
from jax import lax
from jax.experimental import pallas as pl
from jax.experimental.pallas import tpu as pltpu
from jax.sharding import PartitionSpec as P

CP = 32
KJ = 256
MESH = pl.DeviceIdType.MESH


def gather_kernel(n_sec, n_row, cols, img_ref, g_ref, planes, send_sem, recv_sem):
    sec, row = lax.axis_index("sec"), lax.axis_index("row")
    _, rows, width = img_ref.shape
    out_width = width // 2
    wide = cols + 256
    has = {-1: row > 0, 0: None, 1: row < n_row - 1}

    def partners(act):
        for d in (-1, 0, 1):

            def each(d=d):
                for k in range(n_sec):
                    if k or d:
                        act(d, k)

            if d:
                pl.when(has[d])(each)
            else:
                each()

    barrier = pltpu.get_barrier_semaphore()

    def greet(d, k):
        pl.semaphore_signal(
            barrier,
            inc=1,
            device_id=(lax.rem(sec + k, n_sec), row + d),
            device_id_type=MESH,
        )

    partners(greet)

    image = img_ref[0]
    high = image.astype(jnp.bfloat16)
    low = (image - high.astype(jnp.float32)).astype(jnp.bfloat16)
    chunks = width // 256
    stacked = jnp.concatenate(
        [part[:, c * 256 : (c + 1) * 256] for part in (high, low) for c in range(chunks)], axis=0
    )
    source = lax.broadcasted_iota(jnp.int32, (256, 256), 0)
    target = lax.broadcasted_iota(jnp.int32, (256, 256), 1)
    wanted = jnp.where(target < 128, 2 * target, 2 * target - 255)
    pick = jnp.where(source == wanted, 1.0, 0.0).astype(jnp.bfloat16)
    split = jnp.dot(stacked, pick, preferred_element_type=jnp.float32).astype(jnp.bfloat16)
    edge = jnp.zeros((4, rows, 128), jnp.bfloat16)
    planes[:, :, 0:128] = edge
    planes[:, :, 128 + out_width : 256 + out_width] = edge
    for part in range(2):
        for c in range(chunks):
            at = (part * chunks + c) * rows
            for odd in range(2):
                planes[2 * part + odd, :, 128 + c * 128 : 256 + c * 128] = split[
                    at : at + rows, odd * 128 : odd * 128 + 128
                ]

    @pl.when(row == 0)
    def _():
        g_ref[0] = jnp.zeros(g_ref.shape[1:], jnp.bfloat16)

    @pl.when(row == n_row - 1)
    def _():
        g_ref[2] = jnp.zeros(g_ref.shape[1:], jnp.bfloat16)

    up = jnp.where(row > 0, 1, 0)
    down = jnp.where(row < n_row - 1, 1, 0)
    pl.semaphore_wait(barrier, n_sec * (1 + up + down) - 1)

    def window(owner):
        return planes.at[:, :, pl.ds(pl.multiple_of(owner * cols, 128), wide)]

    def outgoing(d, k):
        owner = lax.rem(sec + k, n_sec)
        return pltpu.make_async_remote_copy(
            src_ref=window(owner),
            dst_ref=g_ref.at[1 - d, sec],
            send_sem=send_sem.at[1 - d, k],
            recv_sem=recv_sem.at[1 - d, k],
            device_id=(owner, row + d),
            device_id_type=MESH,
        )

    def incoming(d, k):
        origin = lax.rem(sec + n_sec - k, n_sec)
        return pltpu.make_async_remote_copy(
            src_ref=window(sec),
            dst_ref=g_ref.at[1 + d, origin],
            send_sem=send_sem.at[1 + d, k],
            recv_sem=recv_sem.at[1 + d, k],
            device_id=(origin, row + d),
            device_id_type=MESH,
        )

    partners(lambda d, k: outgoing(d, k).start())
    own = pltpu.make_async_copy(window(sec), g_ref.at[1, sec], send_sem.at[1, 0])
    own.start()
    own.wait()
    partners(lambda d, k: outgoing(d, k).wait_send())
    partners(lambda d, k: incoming(d, k).wait_recv())


def toeplitz(base, reps, step, out_ref):
    for r in range(reps):
        out_ref[r * CP : (r + 1) * CP, :] = (
            pltpu.roll(base, step * r, 1) if r else base
        ).astype(jnp.bfloat16)


def block_kernel(
    n_rows, n_cols, drift_ref, g_ref, stem_ref, b1_ref, b2_ref, bias_ref, out_ref, ts, t1, t2, x1, x2
):
    sec, row = lax.axis_index("sec"), lax.axis_index("row")
    _, sections, _, in_rows, wide = g_ref.shape
    channels, _, out_rows, cols = out_ref.shape
    lanes = cols + 128
    rows_a, rows_h = out_rows + 4, out_rows + 2
    seg1, seg2 = rows_a * CP, rows_h * CP
    high_rows = 3 * in_rows

    stem = stem_ref[...]
    for r in range(rows_a):
        rolled = pltpu.roll(stem, 2 * r, 1) if r else stem
        high = rolled.astype(jnp.bfloat16)
        low = (rolled - high.astype(jnp.float32)).astype(jnp.bfloat16)
        at = slice(r * CP, (r + 1) * CP)
        ts[at, 0:KJ] = high
        ts[at, KJ : 2 * KJ] = high
        ts[at, 2 * KJ : 3 * KJ] = low
    toeplitz(b1_ref[...].astype(jnp.float32), rows_h, CP, t1)
    toeplitz(b2_ref[...].astype(jnp.float32), out_rows, CP, t2)
    nothing = jnp.zeros((3 * seg1, lanes), jnp.bfloat16)
    x1[0 : 3 * seg1, :] = nothing
    x1[(sections + 1) * 3 * seg1 :, :] = nothing
    x2[0 : 3 * seg2, :] = nothing[: 3 * seg2]
    tail = x2.shape[0] - (sections + 1) * 3 * seg2
    x2[(sections + 1) * 3 * seg2 :, :] = nothing[:tail]

    def inside(first, size, limit, axis, repeat, shift=None):
        shape = (size * repeat, 1) if axis == 0 else (1, size)
        pos = lax.broadcasted_iota(jnp.int32, shape, axis)
        pos = (pos // repeat if repeat > 1 else pos) + first
        ok = (pos >= 0) & (pos < limit)
        if shift is not None:
            ok = ok & (pos + shift >= 0) & (pos + shift < limit)
        return jnp.where(ok, 1.0, 0.0)

    def column(which, reps):
        return jnp.concatenate([bias_ref[which, :, 0:1]] * reps, axis=0)

    def spread(value, ref, start, seg):
        for d in range(3):
            moved = pltpu.roll(value, lanes - d, 1) if d else value
            ref[pl.ds(pl.multiple_of(start + d * seg, CP), seg), :] = moved.astype(jnp.bfloat16)

    first_row, first_col = row * out_rows, sec * cols

    def stem_step(s, carry):
        dr, dc = drift_ref[s, 0], drift_ref[s, 1]
        taps = []
        for odd in range(2):
            plane = jnp.concatenate(
                [
                    g_ref[b, s, odd].astype(jnp.float32) + g_ref[b, s, 2 + odd].astype(jnp.float32)
                    for b in range(3)
                ],
                axis=0,
            )
            plane = pltpu.roll(plane, lax.rem(high_rows - 2 * dr, high_rows), 0)
            taps.append(pltpu.roll(plane, wide - 126 - dc, 1))
        even, odd = taps
        shifted = [
            pltpu.roll(even, 1, 1),
            pltpu.roll(odd, 1, 1),
            even,
            odd,
            pltpu.roll(even, wide - 1, 1),
        ]
        field = jnp.concatenate(
            [part[:, :lanes] for part in shifted]
            + [jnp.zeros((KJ - 5 * high_rows, lanes), jnp.float32)],
            axis=0,
        )
        high = field.astype(jnp.bfloat16)
        low = (field - high.astype(jnp.float32)).astype(jnp.bfloat16)
        result = jnp.dot(
            ts[...], jnp.concatenate([high, low, high], axis=0), preferred_element_type=jnp.float32
        )
        result = jnp.maximum(result + column(0, rows_a), 0.0)
        result = result * inside(first_row - 2, rows_a, n_rows, 0, CP, dr)
        result = result * inside(first_col - 2, lanes, n_cols, 1, 1, dc)
        spread(result, x1, (s + 1) * 3 * seg1, seg1)
        return carry

    lax.fori_loop(0, sections, stem_step, 0)

    def first_step(s, carry):
        at = pl.ds(pl.multiple_of(s * 3 * seg1, CP), t1.shape[1])
        result = jnp.dot(t1[...], x1[at, :], preferred_element_type=jnp.float32)
        result = jnp.maximum(result + column(1, rows_h), 0.0)
        result = result * inside(first_row - 1, rows_h, n_rows, 0, CP)
        result = result * inside(first_col - 1, lanes, n_cols, 1, 1)
        spread(result, x2, (s + 1) * 3 * seg2, seg2)
        return carry

    lax.fori_loop(0, sections, first_step, 0)

    def second_step(s, carry):
        at = pl.ds(pl.multiple_of(s * 3 * seg2, CP), t2.shape[1])
        result = jnp.dot(t2[...], x2[at, 0:cols], preferred_element_type=jnp.float32)
        start = (s + 1) * 3 * seg1 + 2 * seg1 + 2 * CP
        kept = x1[pl.ds(pl.multiple_of(start, CP), out_rows * CP), 0:cols]
        result = result + column(2, out_rows) + kept.astype(jnp.float32)
        result = jnp.swapaxes(result.reshape(out_rows, CP, cols), 0, 1)
        out_ref[:, pl.ds(s, 1)] = result[:channels, None].astype(jnp.bfloat16)
        return carry

    lax.fori_loop(0, sections, second_step, 0)


def conv_base(weight, rows, total):
    out, inner = weight.shape[:2]
    base = jnp.transpose(weight, (0, 2, 4, 3, 1))
    base = jnp.pad(base, ((0, CP - out), (0, 0), (0, 0), (0, rows - 3), (0, CP - inner)))
    base = base.reshape(CP, 9 * rows * CP)
    return jnp.pad(base, ((0, 0), (0, total - base.shape[1])))


def on_device(
    n_sec,
    n_row,
    section_image,
    drift_offsets,
    stem_weight,
    stem_bias,
    first_weight,
    first_bias,
    second_weight,
    second_bias,
):
    _, in_rows, width = section_image.shape
    sections = n_sec
    channels = stem_weight.shape[0]
    out_rows, out_width = in_rows // 2, width // 2
    cols = out_width // n_sec
    wide, lanes = cols + 256, cols + 128
    vmem = pl.BlockSpec(memory_space=pltpu.VMEM)
    gathered = pl.pallas_call(
        functools.partial(gather_kernel, n_sec, n_row, cols),
        out_shape=jax.ShapeDtypeStruct((3, sections, 4, in_rows, wide), jnp.bfloat16),
        in_specs=[vmem],
        out_specs=vmem,
        scratch_shapes=[
            pltpu.VMEM((4, in_rows, out_width + 256), jnp.bfloat16),
            pltpu.SemaphoreType.DMA((3, n_sec)),
            pltpu.SemaphoreType.DMA((3, n_sec)),
        ],
        compiler_params=pltpu.CompilerParams(collective_id=0, has_side_effects=True),
        name="gather_image",
    )(section_image)

    k1 = 9 * (out_rows + 4) * CP
    k2 = -(-9 * (out_rows + 2) * CP // 128) * 128
    stem = jnp.transpose(stem_weight[:, 0], (0, 2, 1))
    stem = jnp.pad(stem, ((0, CP - channels), (0, 0), (in_rows - 6, 2 * in_rows + 1)))
    stem = stem.reshape(CP, 15 * in_rows)
    stem = jnp.pad(stem, ((0, 0), (0, KJ - stem.shape[1])))
    biases = jnp.stack([stem_bias, first_bias, second_bias])
    biases = jnp.pad(biases, ((0, 0), (0, CP - channels)))
    biases = jnp.broadcast_to(biases[:, :, None], (3, CP, 128))
    seg1, seg2 = (out_rows + 4) * CP, (out_rows + 2) * CP
    return pl.pallas_call(
        functools.partial(block_kernel, n_row * out_rows, out_width),
        out_shape=jax.ShapeDtypeStruct((channels, sections, out_rows, cols), jnp.bfloat16),
        in_specs=[pl.BlockSpec(memory_space=pltpu.SMEM)] + [vmem] * 5,
        out_specs=vmem,
        scratch_shapes=[
            pltpu.VMEM((seg1, 3 * KJ), jnp.bfloat16),
            pltpu.VMEM((seg2, k1), jnp.bfloat16),
            pltpu.VMEM((out_rows * CP, k2), jnp.bfloat16),
            pltpu.VMEM(((sections + 2) * 3 * seg1, lanes), jnp.bfloat16),
            pltpu.VMEM(((sections + 2) * 3 * seg2 + k2 - 9 * seg2, lanes), jnp.bfloat16),
        ],
        compiler_params=pltpu.CompilerParams(vmem_limit_bytes=48 * 1024 * 1024),
        name="stem_and_block",
    )(
        drift_offsets,
        gathered,
        stem,
        conv_base(first_weight, out_rows + 4, k1),
        conv_base(second_weight, out_rows + 2, k2),
        biases,
    )


def solution(mesh):
    placed = (P("sec", "row", None), P(), P(), P(), P(), P(), P(), P())
    return jax.shard_map(
        functools.partial(on_device, mesh.shape["sec"], mesh.shape["row"]),
        mesh=mesh,
        in_specs=placed,
        out_specs=P(None, None, "row", "sec"),
        check_vma=False,
    )
```

```python
import functools

import jax
import jax.numpy as jnp
from jax import lax
from jax.experimental import pallas as pl
from jax.experimental.pallas import tpu as pltpu
from jax.sharding import PartitionSpec as P

CP = 32
KJ = 256
MESH = pl.DeviceIdType.MESH


def toeplitz(base, reps, step, out_ref):
    for r in range(reps):
        out_ref[r * CP : (r + 1) * CP, :] = (
            pltpu.roll(base, step * r, 1) if r else base
        ).astype(jnp.bfloat16)


def kernel(
    n_sec, n_row, drift_ref, img_ref, stem_ref, w1_ref, w2_ref, bias_ref, out_ref,
    msg, g_ref, base, ts, t1, t2, x1, x2, send_sem, recv_sem, own_sem,
):
    sec, row = lax.axis_index("sec"), lax.axis_index("row")
    _, rows, width = img_ref.shape
    out_width = width // 2
    n_rows, n_cols = n_row * rows // 2, out_width
    cols = out_width // n_sec
    has = {-1: row > 0, 0: None, 1: row < n_row - 1}

    def partners(act):
        for d in (-1, 1, 0):

            def each(d=d):
                for k in range(n_sec):
                    if k or d:
                        act(d, k)

            if d:
                pl.when(has[d])(each)
            else:
                each()

    barrier = pltpu.get_barrier_semaphore()

    def greet(d, k):
        pl.semaphore_signal(
            barrier,
            inc=1,
            device_id=(lax.rem(sec + k, n_sec), row + d),
            device_id_type=MESH,
        )

    partners(greet)

    image = img_ref[0]
    high = image.astype(jnp.bfloat16)
    low = (image - high.astype(jnp.float32)).astype(jnp.bfloat16)
    chunks = width // 256
    stacked = jnp.concatenate(
        [part[:, c * 256 : (c + 1) * 256] for part in (high, low) for c in range(chunks)], axis=0
    )
    source = lax.broadcasted_iota(jnp.int32, (256, 256), 0)
    target = lax.broadcasted_iota(jnp.int32, (256, 256), 1)
    wanted = jnp.where(target < 128, 2 * target, 2 * target - 255)
    pick = jnp.where(source == wanted, 1.0, 0.0).astype(jnp.bfloat16)
    split = jnp.dot(stacked, pick, preferred_element_type=jnp.float32)

    def piece(part, odd, c):
        if c < 0 or c >= chunks:
            return jnp.zeros((rows, 128), jnp.float32)
        at = (part * chunks + c) * rows
        return split[at : at + rows, odd * 128 : odd * 128 + 128]

    lane = lax.broadcasted_iota(jnp.int32, (rows, 128), 1)
    per = cols // 128
    for q in range(n_sec):
        edge = jnp.zeros((rows, 128), jnp.float32)
        for part in range(2):
            for odd in range(2):
                p = 2 * part + odd
                for c in range(per):
                    msg[q, p, :, c * 128 : (c + 1) * 128] = piece(part, odd, q * per + c).astype(
                        jnp.bfloat16
                    )
                left, right = piece(part, odd, q * per - 1), piece(part, odd, (q + 1) * per)
                both = jnp.where(lane >= 120, left, jnp.where(lane < 8, right, 0.0))
                edge = edge + pltpu.roll(both, p * 16 + 8, 1)
        msg[q, 4, :, 0:128] = edge.astype(jnp.bfloat16)
        for c in range(1, per):
            msg[q, 4, :, c * 128 : (c + 1) * 128] = jnp.zeros((rows, 128), jnp.bfloat16)

    @pl.when(row == 0)
    def _():
        g_ref[0] = jnp.zeros(g_ref.shape[1:], jnp.bfloat16)

    @pl.when(row == n_row - 1)
    def _():
        g_ref[2] = jnp.zeros(g_ref.shape[1:], jnp.bfloat16)

    up = jnp.where(row > 0, 1, 0)
    down = jnp.where(row < n_row - 1, 1, 0)
    pl.semaphore_wait(barrier, n_sec * (1 + up + down) - 1)

    def outgoing(d, k):
        owner = lax.rem(sec + k, n_sec)
        return pltpu.make_async_remote_copy(
            src_ref=msg.at[owner],
            dst_ref=g_ref.at[1 - d, sec],
            send_sem=send_sem.at[1 - d, k],
            recv_sem=recv_sem.at[1 - d, k],
            device_id=(owner, row + d),
            device_id_type=MESH,
        )

    def incoming(d, k):
        origin = lax.rem(sec + n_sec - k, n_sec)
        return pltpu.make_async_remote_copy(
            src_ref=msg.at[sec],
            dst_ref=g_ref.at[1 + d, origin],
            send_sem=send_sem.at[1 + d, k],
            recv_sem=recv_sem.at[1 + d, k],
            device_id=(origin, row + d),
            device_id_type=MESH,
        )

    partners(lambda d, k: outgoing(d, k).start())
    own = pltpu.make_async_copy(msg.at[sec], g_ref.at[1, sec], own_sem)
    own.start()

    _, sections, _, in_rows, _ = g_ref.shape
    wide = cols + 256
    channels, _, out_rows, _ = out_ref.shape
    lanes = cols + 128
    rows_a, rows_h = out_rows + 4, out_rows + 2
    seg1, seg2 = rows_a * CP, rows_h * CP
    high_rows = 3 * in_rows

    stem = stem_ref[...]
    for r in range(rows_a):
        rolled = pltpu.roll(stem, 2 * r, 1) if r else stem
        high = rolled.astype(jnp.bfloat16)
        low = (rolled - high.astype(jnp.float32)).astype(jnp.bfloat16)
        at = slice(r * CP, (r + 1) * CP)
        ts[at, 0:KJ] = high
        ts[at, KJ : 2 * KJ] = high
        ts[at, 2 * KJ : 3 * KJ] = low
    for w_ref, seg, reps, ref in ((w1_ref, seg1, rows_h, t1), (w2_ref, seg2, out_rows, t2)):
        base[...] = jnp.zeros(base.shape, jnp.float32)
        for ds in range(3):
            for tap in range(3):
                for dx in range(3):
                    at = (ds * 3 + dx) * seg + tap * CP
                    base[0:channels, at : at + channels] = w_ref[ds, tap, dx].astype(jnp.float32)
        toeplitz(base[:, : ref.shape[1]], reps, CP, ref)
    nothing = jnp.zeros((3 * seg1, lanes), jnp.bfloat16)
    x1[0 : 3 * seg1, :] = nothing
    x1[(sections + 1) * 3 * seg1 :, :] = nothing
    x2[0 : 3 * seg2, :] = nothing[: 3 * seg2]
    tail = x2.shape[0] - (sections + 1) * 3 * seg2
    x2[(sections + 1) * 3 * seg2 :, :] = nothing[:tail]

    def inside(first, size, limit, axis, repeat, shift=None):
        shape = (size * repeat, 1) if axis == 0 else (1, size)
        pos = lax.broadcasted_iota(jnp.int32, shape, axis)
        pos = (pos // repeat if repeat > 1 else pos) + first
        ok = (pos >= 0) & (pos < limit)
        if shift is not None:
            ok = ok & (pos + shift >= 0) & (pos + shift < limit)
        return jnp.where(ok, 1.0, 0.0)

    def column(which, reps):
        return jnp.concatenate([bias_ref[which, :, 0:1]] * reps, axis=0)

    def spread(value, ref, start, seg):
        for d in range(3):
            moved = pltpu.roll(value, lanes - d, 1) if d else value
            ref[pl.ds(pl.multiple_of(start + d * seg, CP), seg), :] = moved.astype(jnp.bfloat16)

    own.wait()
    partners(lambda d, k: incoming(d, k).wait_recv())
    first_row, first_col = row * out_rows, sec * cols

    def stem_step(s, carry):
        dr, dc = drift_ref[s, 0], drift_ref[s, 1]
        taps = []
        for odd in range(2):
            blocks = []
            for b in range(3):
                rim = g_ref[b, s, 4, :, 0:128].astype(jnp.float32)
                total = None
                for p in (odd, 2 + odd):
                    ends = pltpu.roll(rim, 120 - 16 * p, 1)
                    main = g_ref[b, s, p].astype(jnp.float32)
                    part = jnp.concatenate([ends, main, ends], axis=1)
                    total = part if total is None else total + part
                blocks.append(total)
            plane = jnp.concatenate(blocks, axis=0)
            plane = pltpu.roll(plane, lax.rem(high_rows - 2 * dr, high_rows), 0)
            taps.append(pltpu.roll(plane, wide - 126 - dc, 1))
        even, odd = taps
        shifted = [
            pltpu.roll(even, 1, 1),
            pltpu.roll(odd, 1, 1),
            even,
            odd,
            pltpu.roll(even, wide - 1, 1),
        ]
        field = jnp.concatenate(
            [part[:, :lanes] for part in shifted]
            + [jnp.zeros((KJ - 5 * high_rows, lanes), jnp.float32)],
            axis=0,
        )
        high = field.astype(jnp.bfloat16)
        low = (field - high.astype(jnp.float32)).astype(jnp.bfloat16)
        result = jnp.dot(
            ts[...], jnp.concatenate([high, low, high], axis=0), preferred_element_type=jnp.float32
        )
        result = jnp.maximum(result + column(0, rows_a), 0.0)
        result = result * inside(first_row - 2, rows_a, n_rows, 0, CP, dr)
        result = result * inside(first_col - 2, lanes, n_cols, 1, 1, dc)
        spread(result, x1, (s + 1) * 3 * seg1, seg1)
        return carry

    lax.fori_loop(0, sections, stem_step, 0)

    def first_step(s, carry):
        at = pl.ds(pl.multiple_of(s * 3 * seg1, CP), t1.shape[1])
        result = jnp.dot(t1[...], x1[at, :], preferred_element_type=jnp.float32)
        result = jnp.maximum(result + column(1, rows_h), 0.0)
        result = result * inside(first_row - 1, rows_h, n_rows, 0, CP)
        result = result * inside(first_col - 1, lanes, n_cols, 1, 1)
        spread(result, x2, (s + 1) * 3 * seg2, seg2)
        return carry

    lax.fori_loop(0, sections, first_step, 0)

    def second_step(s, carry):
        at = pl.ds(pl.multiple_of(s * 3 * seg2, CP), t2.shape[1])
        result = jnp.dot(t2[...], x2[at, 0:cols], preferred_element_type=jnp.float32)
        start = (s + 1) * 3 * seg1 + 2 * seg1 + 2 * CP
        kept = x1[pl.ds(pl.multiple_of(start, CP), out_rows * CP), 0:cols]
        result = result + column(2, out_rows) + kept.astype(jnp.float32)
        result = jnp.swapaxes(result.reshape(out_rows, CP, cols), 0, 1)
        out_ref[:, pl.ds(s, 1)] = result[:channels, None].astype(jnp.bfloat16)
        return carry

    lax.fori_loop(0, sections, second_step, 0)
    partners(lambda d, k: outgoing(d, k).wait_send())


def on_device(
    n_sec,
    n_row,
    section_image,
    drift_offsets,
    stem_weight,
    stem_bias,
    first_weight,
    first_bias,
    second_weight,
    second_bias,
):
    _, in_rows, width = section_image.shape
    sections = n_sec
    channels = stem_weight.shape[0]
    out_rows, out_width = in_rows // 2, width // 2
    cols = out_width // n_sec
    lanes = cols + 128
    vmem = pl.BlockSpec(memory_space=pltpu.VMEM)
    k1 = 9 * (out_rows + 4) * CP
    k2 = -(-9 * (out_rows + 2) * CP // 128) * 128
    stem = jnp.transpose(stem_weight[:, 0], (0, 2, 1))
    stem = jnp.pad(stem, ((0, CP - channels), (0, 0), (in_rows - 6, 2 * in_rows + 1)))
    stem = stem.reshape(CP, 15 * in_rows)
    stem = jnp.pad(stem, ((0, 0), (0, KJ - stem.shape[1])))
    biases = jnp.stack([stem_bias, first_bias, second_bias])
    biases = jnp.pad(biases, ((0, 0), (0, CP - channels)))
    biases = jnp.broadcast_to(biases[:, :, None], (3, CP, 128))
    seg1, seg2 = (out_rows + 4) * CP, (out_rows + 2) * CP
    return pl.pallas_call(
        functools.partial(kernel, n_sec, n_row),
        out_shape=jax.ShapeDtypeStruct((channels, sections, out_rows, cols), jnp.bfloat16),
        in_specs=[pl.BlockSpec(memory_space=pltpu.SMEM)] + [vmem] * 5,
        out_specs=vmem,
        scratch_shapes=[
            pltpu.VMEM((n_sec, 5, in_rows, cols), jnp.bfloat16),
            pltpu.VMEM((3, sections, 5, in_rows, cols), jnp.bfloat16),
            pltpu.VMEM((CP, max(k1, k2)), jnp.float32),
            pltpu.VMEM((seg1, 3 * KJ), jnp.bfloat16),
            pltpu.VMEM((seg2, k1), jnp.bfloat16),
            pltpu.VMEM((out_rows * CP, k2), jnp.bfloat16),
            pltpu.VMEM(((sections + 2) * 3 * seg1, lanes), jnp.bfloat16),
            pltpu.VMEM(((sections + 2) * 3 * seg2 + k2 - 9 * seg2, lanes), jnp.bfloat16),
            pltpu.SemaphoreType.DMA((3, n_sec)),
            pltpu.SemaphoreType.DMA((3, n_sec)),
            pltpu.SemaphoreType.DMA,
        ],
        compiler_params=pltpu.CompilerParams(
            collective_id=0, has_side_effects=True, vmem_limit_bytes=48 * 1024 * 1024
        ),
        name="section_block",
    )(
        drift_offsets,
        section_image,
        stem,
        jnp.transpose(first_weight, (2, 3, 4, 0, 1)),
        jnp.transpose(second_weight, (2, 3, 4, 0, 1)),
        biases,
    )


def solution(mesh):
    placed = (P("sec", "row", None), P(), P(), P(), P(), P(), P(), P())
    return jax.shard_map(
        functools.partial(on_device, mesh.shape["sec"], mesh.shape["row"]),
        mesh=mesh,
        in_specs=placed,
        out_specs=P(None, None, "row", "sec"),
        check_vma=False,
    )
```

```python
import functools

import jax
import jax.numpy as jnp
from jax import lax
from jax.experimental import pallas as pl
from jax.experimental.pallas import tpu as pltpu
from jax.sharding import PartitionSpec as P

CP = 32
KJ = 256
MESH = pl.DeviceIdType.MESH


def toeplitz(base, reps, step, out_ref):
    for r in range(reps):
        out_ref[r * CP : (r + 1) * CP, :] = (
            pltpu.roll(base, step * r, 1) if r else base
        ).astype(jnp.bfloat16)


def kernel(
    n_sec, n_row, drift_ref, img_hbm, stem_hbm, w1_hbm, w2_hbm, sb_hbm, fb_hbm, cb_hbm, out_ref,
    img_ref, stem_ref, w1_ref, w2_ref, bias_rows, bias_ref,
    msg, g_ref, base, ts, t1, t2, x1, x2, send_sem, recv_sem, own_sem, in_sem,
):
    sec, row = lax.axis_index("sec"), lax.axis_index("row")
    _, rows, width = img_ref.shape
    out_width = width // 2
    n_rows, n_cols = n_row * rows // 2, out_width
    cols = out_width // n_sec
    has = {-1: row > 0, 0: None, 1: row < n_row - 1}

    def partners(act):
        for k in range(n_sec):
            for d in (-1, 1, 0):
                if d:
                    pl.when(has[d])(functools.partial(act, d, k))
                elif k:
                    act(d, k)

    loads = [
        pltpu.make_async_copy(source, target, in_sem.at[i])
        for i, (source, target) in enumerate(
            (
                (img_hbm, img_ref),
                (stem_hbm, stem_ref),
                (sb_hbm, bias_rows.at[0]),
                (fb_hbm, bias_rows.at[1]),
                (cb_hbm, bias_rows.at[2]),
                (w1_hbm, w1_ref),
                (w2_hbm, w2_ref),
            )
        )
    ]
    for load in loads:
        load.start()
    barrier = pltpu.get_barrier_semaphore()

    def greet(d, k):
        pl.semaphore_signal(
            barrier,
            inc=1,
            device_id=(lax.rem(sec + k, n_sec), row + d),
            device_id_type=MESH,
        )

    partners(greet)

    loads[0].wait()
    image = img_ref[0]
    high = image.astype(jnp.bfloat16)
    low = (image - high.astype(jnp.float32)).astype(jnp.bfloat16)
    chunks = width // 256
    stacked = jnp.concatenate(
        [part[:, c * 256 : (c + 1) * 256] for part in (high, low) for c in range(chunks)], axis=0
    )
    source = lax.broadcasted_iota(jnp.int32, (256, 256), 0)
    target = lax.broadcasted_iota(jnp.int32, (256, 256), 1)
    wanted = jnp.where(target < 128, 2 * target, 2 * target - 255)
    pick = jnp.where(source == wanted, 1.0, 0.0).astype(jnp.bfloat16)
    split = jnp.dot(stacked, pick, preferred_element_type=jnp.float32)

    def piece(part, odd, c):
        if c < 0 or c >= chunks:
            return jnp.zeros((rows, 128), jnp.float32)
        at = (part * chunks + c) * rows
        return split[at : at + rows, odd * 128 : odd * 128 + 128]

    lane = lax.broadcasted_iota(jnp.int32, (rows, 128), 1)
    per = cols // 128
    for q in range(n_sec):
        edge = jnp.zeros((rows, 128), jnp.float32)
        for part in range(2):
            for odd in range(2):
                p = 2 * part + odd
                for c in range(per):
                    msg[q, p, :, c * 128 : (c + 1) * 128] = piece(part, odd, q * per + c).astype(
                        jnp.bfloat16
                    )
                left, right = piece(part, odd, q * per - 1), piece(part, odd, (q + 1) * per)
                both = jnp.where(lane >= 120, left, jnp.where(lane < 8, right, 0.0))
                edge = edge + pltpu.roll(both, p * 16 + 8, 1)
        msg[q, 4, :, 0:128] = edge.astype(jnp.bfloat16)
        for c in range(1, per):
            msg[q, 4, :, c * 128 : (c + 1) * 128] = jnp.zeros((rows, 128), jnp.bfloat16)

    @pl.when(row == 0)
    def _():
        g_ref[0] = jnp.zeros(g_ref.shape[1:], jnp.bfloat16)

    @pl.when(row == n_row - 1)
    def _():
        g_ref[2] = jnp.zeros(g_ref.shape[1:], jnp.bfloat16)

    up = jnp.where(row > 0, 1, 0)
    down = jnp.where(row < n_row - 1, 1, 0)
    pl.semaphore_wait(barrier, n_sec * (1 + up + down) - 1)

    def outgoing(d, k):
        owner = lax.rem(sec + k, n_sec)
        return pltpu.make_async_remote_copy(
            src_ref=msg.at[owner],
            dst_ref=g_ref.at[1 - d, sec],
            send_sem=send_sem.at[1 - d, k],
            recv_sem=recv_sem.at[1 - d, k],
            device_id=(owner, row + d),
            device_id_type=MESH,
        )

    def incoming(d, k):
        origin = lax.rem(sec + n_sec - k, n_sec)
        return pltpu.make_async_remote_copy(
            src_ref=msg.at[sec],
            dst_ref=g_ref.at[1 + d, origin],
            send_sem=send_sem.at[1 + d, k],
            recv_sem=recv_sem.at[1 + d, k],
            device_id=(origin, row + d),
            device_id_type=MESH,
        )

    partners(lambda d, k: outgoing(d, k).start())
    own = pltpu.make_async_copy(msg.at[sec], g_ref.at[1, sec], own_sem)
    own.start()

    _, sections, _, in_rows, _ = g_ref.shape
    wide = cols + 256
    channels, _, out_rows, _ = out_ref.shape
    lanes = cols + 128
    rows_a, rows_h = out_rows + 4, out_rows + 2
    seg1, seg2 = rows_a * CP, rows_h * CP
    high_rows = 3 * in_rows

    for load in loads[1:]:
        load.wait()
    parts = [stem_ref[i, j] for i in range(5) for j in range(5)] + [bias_rows[b] for b in range(3)]
    parts.append(jnp.zeros((4, channels), jnp.float32))
    small = jnp.concatenate(parts, axis=0)
    item = lax.broadcasted_iota(jnp.int32, (32, KJ + 384), 0)
    place = lax.broadcasted_iota(jnp.int32, (32, KJ + 384), 1)
    tap_i, tap_j = item // 5, item % 5
    spot = tap_j * high_rows + in_rows - 6 + tap_i
    hit = ((item < 25) & (place < KJ) & (place == spot)) | (
        (item >= 25) & (place >= KJ) & ((place - KJ) // 128 == item - 25)
    )
    laid = lax.dot_general(
        small,
        jnp.where(hit, 1.0, 0.0),
        (((0,), (0,)), ((), ())),
        precision=lax.Precision.HIGHEST,
        preferred_element_type=jnp.float32,
    )
    laid = jnp.concatenate([laid, jnp.zeros((CP - channels, KJ + 384), jnp.float32)], axis=0)
    stem = laid[:, :KJ]
    for b in range(3):
        bias_ref[b] = laid[:, KJ + b * 128 : KJ + (b + 1) * 128]
    for r in range(rows_a):
        rolled = pltpu.roll(stem, 2 * r, 1) if r else stem
        high = rolled.astype(jnp.bfloat16)
        low = (rolled - high.astype(jnp.float32)).astype(jnp.bfloat16)
        at = slice(r * CP, (r + 1) * CP)
        ts[at, 0:KJ] = high
        ts[at, KJ : 2 * KJ] = high
        ts[at, 2 * KJ : 3 * KJ] = low
    for w_ref, seg, reps, ref in ((w1_ref, seg1, rows_h, t1), (w2_ref, seg2, out_rows, t2)):
        base[...] = jnp.zeros(base.shape, jnp.float32)
        for ds in range(3):
            for tap in range(3):
                for dx in range(3):
                    at = (ds * 3 + dx) * seg + tap * CP
                    base[0:channels, at : at + channels] = w_ref[ds, tap, dx].astype(jnp.float32)
        toeplitz(base[:, : ref.shape[1]], reps, CP, ref)
    nothing = jnp.zeros((3 * seg1, lanes), jnp.bfloat16)
    x1[0 : 3 * seg1, :] = nothing
    x1[(sections + 1) * 3 * seg1 :, :] = nothing
    x2[0 : 3 * seg2, :] = nothing[: 3 * seg2]
    tail = x2.shape[0] - (sections + 1) * 3 * seg2
    x2[(sections + 1) * 3 * seg2 :, :] = nothing[:tail]

    def inside(first, size, limit, axis, repeat, shift=None):
        shape = (size * repeat, 1) if axis == 0 else (1, size)
        pos = lax.broadcasted_iota(jnp.int32, shape, axis)
        pos = (pos // repeat if repeat > 1 else pos) + first
        ok = (pos >= 0) & (pos < limit)
        if shift is not None:
            ok = ok & (pos + shift >= 0) & (pos + shift < limit)
        return jnp.where(ok, 1.0, 0.0)

    def column(which, reps):
        return jnp.concatenate([bias_ref[which, :, 0:1]] * reps, axis=0)

    def spread(value, ref, start, seg):
        for d in range(3):
            moved = pltpu.roll(value, lanes - d, 1) if d else value
            ref[pl.ds(pl.multiple_of(start + d * seg, CP), seg), :] = moved.astype(jnp.bfloat16)

    own.wait()
    first_row, first_col = row * out_rows, sec * cols

    def stem_step(k, carry):
        s = lax.rem(sec + n_sec - k, n_sec)
        for d, there in ((-1, has[-1]), (1, has[1]), (0, k > 0)):
            pl.when(there)(lambda d=d: incoming(d, k).wait_recv())
        dr, dc = drift_ref[0, s], drift_ref[1, s]
        taps = []
        for odd in range(2):
            blocks = []
            for b in range(3):
                rim = g_ref[b, s, 4, :, 0:128].astype(jnp.float32)
                total = None
                for p in (odd, 2 + odd):
                    ends = pltpu.roll(rim, 120 - 16 * p, 1)
                    main = g_ref[b, s, p].astype(jnp.float32)
                    part = jnp.concatenate([ends, main, ends], axis=1)
                    total = part if total is None else total + part
                blocks.append(total)
            plane = jnp.concatenate(blocks, axis=0)
            plane = pltpu.roll(plane, lax.rem(high_rows - 2 * dr, high_rows), 0)
            taps.append(pltpu.roll(plane, wide - 126 - dc, 1))
        even, odd = taps
        shifted = [
            pltpu.roll(even, 1, 1),
            pltpu.roll(odd, 1, 1),
            even,
            odd,
            pltpu.roll(even, wide - 1, 1),
        ]
        field = jnp.concatenate(
            [part[:, :lanes] for part in shifted]
            + [jnp.zeros((KJ - 5 * high_rows, lanes), jnp.float32)],
            axis=0,
        )
        high = field.astype(jnp.bfloat16)
        low = (field - high.astype(jnp.float32)).astype(jnp.bfloat16)
        result = jnp.dot(
            ts[...], jnp.concatenate([high, low, high], axis=0), preferred_element_type=jnp.float32
        )
        result = jnp.maximum(result + column(0, rows_a), 0.0)
        result = result * inside(first_row - 2, rows_a, n_rows, 0, CP, dr)
        result = result * inside(first_col - 2, lanes, n_cols, 1, 1, dc)
        spread(result, x1, (s + 1) * 3 * seg1, seg1)
        return carry

    lax.fori_loop(0, sections, stem_step, 0)

    def first_step(s, carry):
        at = pl.ds(pl.multiple_of(s * 3 * seg1, CP), t1.shape[1])
        result = jnp.dot(t1[...], x1[at, :], preferred_element_type=jnp.float32)
        result = jnp.maximum(result + column(1, rows_h), 0.0)
        result = result * inside(first_row - 1, rows_h, n_rows, 0, CP)
        result = result * inside(first_col - 1, lanes, n_cols, 1, 1)
        spread(result, x2, (s + 1) * 3 * seg2, seg2)
        return carry

    lax.fori_loop(0, sections, first_step, 0)

    def second_step(s, carry):
        at = pl.ds(pl.multiple_of(s * 3 * seg2, CP), t2.shape[1])
        result = jnp.dot(t2[...], x2[at, 0:cols], preferred_element_type=jnp.float32)
        start = (s + 1) * 3 * seg1 + 2 * seg1 + 2 * CP
        kept = x1[pl.ds(pl.multiple_of(start, CP), out_rows * CP), 0:cols]
        result = result + column(2, out_rows) + kept.astype(jnp.float32)
        result = jnp.swapaxes(result.reshape(out_rows, CP, cols), 0, 1)
        out_ref[:, pl.ds(s, 1)] = result[:channels, None].astype(jnp.bfloat16)
        return carry

    lax.fori_loop(0, sections, second_step, 0)
    partners(lambda d, k: outgoing(d, k).wait_send())


def on_device(
    n_sec,
    n_row,
    section_image,
    drift_offsets,
    stem_weight,
    stem_bias,
    first_weight,
    first_bias,
    second_weight,
    second_bias,
):
    _, in_rows, width = section_image.shape
    sections = n_sec
    channels = stem_weight.shape[0]
    out_rows, out_width = in_rows // 2, width // 2
    cols = out_width // n_sec
    lanes = cols + 128
    vmem = pl.BlockSpec(memory_space=pltpu.VMEM)
    k1 = 9 * (out_rows + 4) * CP
    k2 = -(-9 * (out_rows + 2) * CP // 128) * 128
    seg1, seg2 = (out_rows + 4) * CP, (out_rows + 2) * CP
    return pl.pallas_call(
        functools.partial(kernel, n_sec, n_row),
        out_shape=jax.ShapeDtypeStruct((channels, sections, out_rows, cols), jnp.bfloat16),
        in_specs=[pl.BlockSpec(memory_space=pltpu.SMEM)] + [pl.BlockSpec(memory_space=pltpu.HBM)] * 7,
        out_specs=vmem,
        scratch_shapes=[
            pltpu.VMEM(section_image.shape, jnp.float32),
            pltpu.VMEM((5, 5, 1, channels), jnp.float32),
            pltpu.VMEM((3, 3, 3, channels, channels), jnp.bfloat16),
            pltpu.VMEM((3, 3, 3, channels, channels), jnp.bfloat16),
            pltpu.VMEM((3, 1, channels), jnp.float32),
            pltpu.VMEM((3, CP, 128), jnp.float32),
            pltpu.VMEM((n_sec, 5, in_rows, cols), jnp.bfloat16),
            pltpu.VMEM((3, sections, 5, in_rows, cols), jnp.bfloat16),
            pltpu.VMEM((CP, max(k1, k2)), jnp.float32),
            pltpu.VMEM((seg1, 3 * KJ), jnp.bfloat16),
            pltpu.VMEM((seg2, k1), jnp.bfloat16),
            pltpu.VMEM((out_rows * CP, k2), jnp.bfloat16),
            pltpu.VMEM(((sections + 2) * 3 * seg1, lanes), jnp.bfloat16),
            pltpu.VMEM(((sections + 2) * 3 * seg2 + k2 - 9 * seg2, lanes), jnp.bfloat16),
            pltpu.SemaphoreType.DMA((3, n_sec)),
            pltpu.SemaphoreType.DMA((3, n_sec)),
            pltpu.SemaphoreType.DMA,
            pltpu.SemaphoreType.DMA((7,)),
        ],
        compiler_params=pltpu.CompilerParams(
            collective_id=0, has_side_effects=True, vmem_limit_bytes=60 * 1024 * 1024
        ),
        name="section_block",
    )(
        drift_offsets.T,
        section_image,
        jnp.transpose(stem_weight, (2, 3, 1, 0)),
        jnp.transpose(first_weight, (2, 3, 4, 0, 1)),
        jnp.transpose(second_weight, (2, 3, 4, 0, 1)),
        stem_bias[None],
        first_bias[None],
        second_bias[None],
    )


def solution(mesh):
    placed = (P("sec", "row", None), P(), P(), P(), P(), P(), P(), P())
    return jax.shard_map(
        functools.partial(on_device, mesh.shape["sec"], mesh.shape["row"]),
        mesh=mesh,
        in_specs=placed,
        out_specs=P(None, None, "row", "sec"),
        check_vma=False,
    )
```

```python
import functools

import jax
import jax.numpy as jnp
from jax import lax
from jax.experimental import pallas as pl
from jax.experimental.pallas import tpu as pltpu
from jax.sharding import PartitionSpec as P

CP = 32
KJ = 256
MESH = pl.DeviceIdType.MESH


def toeplitz(base, reps, step, out_ref):
    for r in range(reps):
        out_ref[r * CP : (r + 1) * CP, :] = (
            pltpu.roll(base, step * r, 1) if r else base
        ).astype(jnp.bfloat16)


def kernel(
    n_sec, n_row, drift_ref, img_hbm, stem_hbm, w1_hbm, w2_hbm, sb_hbm, fb_hbm, cb_hbm, out_ref,
    img_ref, stem_ref, w1_ref, w2_ref, bias_rows, bias_ref,
    msg, g_ref, base, ts, t1, t2, x1, x2, send_sem, recv_sem, own_sem, in_sem,
):
    sec, row = lax.axis_index("sec"), lax.axis_index("row")
    _, rows, width = img_ref.shape
    out_width = width // 2
    n_rows, n_cols = n_row * rows // 2, out_width
    cols = out_width // n_sec
    has = {-1: row > 0, 0: None, 1: row < n_row - 1}

    def partners(act):
        for k in range(n_sec):
            for d in (-1, 1, 0):
                if d:
                    pl.when(has[d])(functools.partial(act, d, k))
                elif k:
                    act(d, k)

    loads = [
        pltpu.make_async_copy(source, target, in_sem.at[i])
        for i, (source, target) in enumerate(
            (
                (img_hbm, img_ref),
                (stem_hbm, stem_ref),
                (sb_hbm, bias_rows.at[0]),
                (fb_hbm, bias_rows.at[1]),
                (cb_hbm, bias_rows.at[2]),
                (w1_hbm, w1_ref),
                (w2_hbm, w2_ref),
            )
        )
    ]
    for load in loads:
        load.start()
    barrier = pltpu.get_barrier_semaphore()

    def greet(d, k):
        pl.semaphore_signal(
            barrier,
            inc=1,
            device_id=(lax.rem(sec + k, n_sec), row + d),
            device_id_type=MESH,
        )

    partners(greet)

    loads[0].wait()
    image = img_ref[0]
    high = image.astype(jnp.bfloat16)
    low = (image - high.astype(jnp.float32)).astype(jnp.bfloat16)
    chunks = width // 256
    stacked = jnp.concatenate(
        [part[:, c * 256 : (c + 1) * 256] for part in (high, low) for c in range(chunks)], axis=0
    )
    source = lax.broadcasted_iota(jnp.int32, (256, 256), 0)
    target = lax.broadcasted_iota(jnp.int32, (256, 256), 1)
    wanted = jnp.where(target < 128, 2 * target, 2 * target - 255)
    pick = jnp.where(source == wanted, 1.0, 0.0).astype(jnp.bfloat16)
    split = jnp.dot(stacked, pick, preferred_element_type=jnp.float32)

    def piece(part, odd, c):
        if c < 0 or c >= chunks:
            return jnp.zeros((rows, 128), jnp.float32)
        at = (part * chunks + c) * rows
        return split[at : at + rows, odd * 128 : odd * 128 + 128]

    lane = lax.broadcasted_iota(jnp.int32, (rows, 128), 1)
    per = cols // 128
    for q in range(n_sec):
        edge = jnp.zeros((rows, 128), jnp.float32)
        for part in range(2):
            for odd in range(2):
                p = 2 * part + odd
                for c in range(per):
                    msg[q, p, :, c * 128 : (c + 1) * 128] = piece(part, odd, q * per + c).astype(
                        jnp.bfloat16
                    )
                left, right = piece(part, odd, q * per - 1), piece(part, odd, (q + 1) * per)
                both = jnp.where(lane >= 120, left, jnp.where(lane < 8, right, 0.0))
                edge = edge + pltpu.roll(both, p * 16 + 8, 1)
        msg[q, 4, :, 0:128] = edge.astype(jnp.bfloat16)
        for c in range(1, per):
            msg[q, 4, :, c * 128 : (c + 1) * 128] = jnp.zeros((rows, 128), jnp.bfloat16)

    @pl.when(row == 0)
    def _():
        g_ref[0] = jnp.zeros(g_ref.shape[1:], jnp.bfloat16)

    @pl.when(row == n_row - 1)
    def _():
        g_ref[2] = jnp.zeros(g_ref.shape[1:], jnp.bfloat16)

    up = jnp.where(row > 0, 1, 0)
    down = jnp.where(row < n_row - 1, 1, 0)
    pl.semaphore_wait(barrier, n_sec * (1 + up + down) - 1)

    def outgoing(d, k):
        owner = lax.rem(sec + k, n_sec)
        return pltpu.make_async_remote_copy(
            src_ref=msg.at[owner],
            dst_ref=g_ref.at[1 - d, sec],
            send_sem=send_sem.at[1 - d, k],
            recv_sem=recv_sem.at[1 - d, k],
            device_id=(owner, row + d),
            device_id_type=MESH,
        )

    def incoming(d, k):
        origin = lax.rem(sec + n_sec - k, n_sec)
        return pltpu.make_async_remote_copy(
            src_ref=msg.at[sec],
            dst_ref=g_ref.at[1 + d, origin],
            send_sem=send_sem.at[1 + d, k],
            recv_sem=recv_sem.at[1 + d, k],
            device_id=(origin, row + d),
            device_id_type=MESH,
        )

    partners(lambda d, k: outgoing(d, k).start())
    own = pltpu.make_async_copy(msg.at[sec], g_ref.at[1, sec], own_sem)
    own.start()

    _, sections, _, in_rows, _ = g_ref.shape
    wide = cols + 256
    channels, _, out_rows, _ = out_ref.shape
    lanes = cols + 128
    rows_a, rows_h = out_rows + 4, out_rows + 2
    seg1, seg2 = rows_a * CP, rows_h * CP
    high_rows = 3 * in_rows

    for load in loads[1:]:
        load.wait()
    parts = [stem_ref[i, j] for i in range(5) for j in range(5)] + [bias_rows[b] for b in range(3)]
    parts.append(jnp.zeros((4, channels), jnp.float32))
    small = jnp.concatenate(parts, axis=0)
    item = lax.broadcasted_iota(jnp.int32, (32, KJ + 384), 0)
    place = lax.broadcasted_iota(jnp.int32, (32, KJ + 384), 1)
    tap_i, tap_j = item // 5, item % 5
    spot = tap_j * high_rows + in_rows - 6 + tap_i
    hit = ((item < 25) & (place < KJ) & (place == spot)) | (
        (item >= 25) & (place >= KJ) & ((place - KJ) // 128 == item - 25)
    )
    laid = lax.dot_general(
        small,
        jnp.where(hit, 1.0, 0.0),
        (((0,), (0,)), ((), ())),
        precision=lax.Precision.HIGHEST,
        preferred_element_type=jnp.float32,
    )
    laid = jnp.concatenate([laid, jnp.zeros((CP - channels, KJ + 384), jnp.float32)], axis=0)
    stem = laid[:, :KJ]
    for b in range(3):
        bias_ref[b] = laid[:, KJ + b * 128 : KJ + (b + 1) * 128]
    for r in range(rows_a):
        rolled = pltpu.roll(stem, 2 * r, 1) if r else stem
        high = rolled.astype(jnp.bfloat16)
        low = (rolled - high.astype(jnp.float32)).astype(jnp.bfloat16)
        at = slice(r * CP, (r + 1) * CP)
        ts[at, 0:KJ] = high
        ts[at, KJ : 2 * KJ] = high
        ts[at, 2 * KJ : 3 * KJ] = low
    for w_ref, seg, reps, ref in ((w1_ref, seg1, rows_h, t1), (w2_ref, seg2, out_rows, t2)):
        base[...] = jnp.zeros(base.shape, jnp.float32)
        for ds in range(3):
            for tap in range(3):
                for dx in range(3):
                    at = (ds * 3 + dx) * seg + tap * CP
                    base[0:channels, at : at + channels] = w_ref[ds, tap, dx].astype(jnp.float32)
        toeplitz(base[:, : ref.shape[1]], reps, CP, ref)
    nothing = jnp.zeros((3 * seg1, lanes), jnp.bfloat16)
    x1[0 : 3 * seg1, :] = nothing
    x1[(sections + 1) * 3 * seg1 :, :] = nothing
    x2[0 : 3 * seg2, :] = nothing[: 3 * seg2]
    tail = x2.shape[0] - (sections + 1) * 3 * seg2
    x2[(sections + 1) * 3 * seg2 :, :] = nothing[:tail]

    def inside(first, size, limit, axis, repeat, shift=None):
        shape = (size * repeat, 1) if axis == 0 else (1, size)
        pos = lax.broadcasted_iota(jnp.int32, shape, axis)
        pos = (pos // repeat if repeat > 1 else pos) + first
        ok = (pos >= 0) & (pos < limit)
        if shift is not None:
            ok = ok & (pos + shift >= 0) & (pos + shift < limit)
        return jnp.where(ok, 1.0, 0.0)

    def column(which, reps):
        return jnp.concatenate([bias_ref[which, :, 0:1]] * reps, axis=0)

    def spread(value, ref, start, seg):
        for d in range(3):
            moved = pltpu.roll(value, lanes - d, 1) if d else value
            ref[pl.ds(pl.multiple_of(start + d * seg, CP), seg), :] = moved.astype(jnp.bfloat16)

    own.wait()
    first_row, first_col = row * out_rows, sec * cols

    def stem_step(k, carry):
        s = lax.rem(sec + n_sec - k, n_sec)
        for d, there in ((-1, has[-1]), (1, has[1]), (0, k > 0)):
            pl.when(there)(lambda d=d: incoming(d, k).wait_recv())
        dr, dc = drift_ref[0, s], drift_ref[1, s]
        taps = []
        for odd in range(2):
            blocks = []
            for b in range(3):
                rim = g_ref[b, s, 4, :, 0:128].astype(jnp.float32)
                total = None
                for p in (odd, 2 + odd):
                    ends = pltpu.roll(rim, 120 - 16 * p, 1)
                    main = g_ref[b, s, p].astype(jnp.float32)
                    part = jnp.concatenate([ends, main, ends], axis=1)
                    total = part if total is None else total + part
                blocks.append(total)
            plane = jnp.concatenate(blocks, axis=0)
            plane = pltpu.roll(plane, lax.rem(high_rows - 2 * dr, high_rows), 0)
            taps.append(pltpu.roll(plane, wide - 126 - dc, 1))
        even, odd = taps
        shifted = [
            pltpu.roll(even, 1, 1),
            pltpu.roll(odd, 1, 1),
            even,
            odd,
            pltpu.roll(even, wide - 1, 1),
        ]
        field = jnp.concatenate(
            [part[:, :lanes] for part in shifted]
            + [jnp.zeros((KJ - 5 * high_rows, lanes), jnp.float32)],
            axis=0,
        )
        high = field.astype(jnp.bfloat16)
        low = (field - high.astype(jnp.float32)).astype(jnp.bfloat16)
        result = jnp.dot(
            ts[...], jnp.concatenate([high, low, high], axis=0), preferred_element_type=jnp.float32
        )
        result = jnp.maximum(result + column(0, rows_a), 0.0)
        result = result * inside(first_row - 2, rows_a, n_rows, 0, CP, dr)
        result = result * inside(first_col - 2, lanes, n_cols, 1, 1, dc)
        spread(result, x1, (s + 1) * 3 * seg1, seg1)
        return carry

    lax.fori_loop(0, sections, stem_step, 0)

    def first_step(s, carry):
        at = pl.ds(pl.multiple_of(s * 3 * seg1, CP), t1.shape[1])
        result = jnp.dot(t1[...], x1[at, :], preferred_element_type=jnp.float32)
        result = jnp.maximum(result + column(1, rows_h), 0.0)
        result = result * inside(first_row - 1, rows_h, n_rows, 0, CP)
        result = result * inside(first_col - 1, lanes, n_cols, 1, 1)
        spread(result, x2, (s + 1) * 3 * seg2, seg2)
        return carry

    lax.fori_loop(0, sections, first_step, 0)

    def second_step(s, carry):
        at = pl.ds(pl.multiple_of(s * 3 * seg2, CP), t2.shape[1])
        result = jnp.dot(t2[...], x2[at, 0:cols], preferred_element_type=jnp.float32)
        start = (s + 1) * 3 * seg1 + 2 * seg1 + 2 * CP
        kept = x1[pl.ds(pl.multiple_of(start, CP), out_rows * CP), 0:cols]
        result = result + column(2, out_rows) + kept.astype(jnp.float32)
        result = jnp.swapaxes(result.reshape(out_rows, CP, cols), 0, 1)
        out_ref[:, pl.ds(s, 1)] = result[:channels, None].astype(jnp.bfloat16)
        return carry

    lax.fori_loop(0, sections, second_step, 0)
    partners(lambda d, k: outgoing(d, k).wait_send())


def on_device(
    n_sec,
    n_row,
    section_image,
    drift_offsets,
    stem_weight,
    stem_bias,
    first_weight,
    first_bias,
    second_weight,
    second_bias,
):
    _, in_rows, width = section_image.shape
    sections = n_sec
    channels = stem_weight.shape[0]
    out_rows, out_width = in_rows // 2, width // 2
    cols = out_width // n_sec
    lanes = cols + 128
    vmem = pl.BlockSpec(memory_space=pltpu.VMEM)
    k1 = 9 * (out_rows + 4) * CP
    k2 = -(-9 * (out_rows + 2) * CP // 128) * 128
    seg1, seg2 = (out_rows + 4) * CP, (out_rows + 2) * CP
    return pl.pallas_call(
        functools.partial(kernel, n_sec, n_row),
        out_shape=pltpu.VMEM((channels, sections, out_rows, cols), jnp.bfloat16),
        in_specs=[pl.BlockSpec(memory_space=pltpu.SMEM)] + [pl.BlockSpec(memory_space=pltpu.HBM)] * 7,
        out_specs=vmem,
        scratch_shapes=[
            pltpu.VMEM(section_image.shape, jnp.float32),
            pltpu.VMEM((5, 5, 1, channels), jnp.float32),
            pltpu.VMEM((3, 3, 3, channels, channels), jnp.bfloat16),
            pltpu.VMEM((3, 3, 3, channels, channels), jnp.bfloat16),
            pltpu.VMEM((3, 1, channels), jnp.float32),
            pltpu.VMEM((3, CP, 128), jnp.float32),
            pltpu.VMEM((n_sec, 5, in_rows, cols), jnp.bfloat16),
            pltpu.VMEM((3, sections, 5, in_rows, cols), jnp.bfloat16),
            pltpu.VMEM((CP, max(k1, k2)), jnp.float32),
            pltpu.VMEM((seg1, 3 * KJ), jnp.bfloat16),
            pltpu.VMEM((seg2, k1), jnp.bfloat16),
            pltpu.VMEM((out_rows * CP, k2), jnp.bfloat16),
            pltpu.VMEM(((sections + 2) * 3 * seg1, lanes), jnp.bfloat16),
            pltpu.VMEM(((sections + 2) * 3 * seg2 + k2 - 9 * seg2, lanes), jnp.bfloat16),
            pltpu.SemaphoreType.DMA((3, n_sec)),
            pltpu.SemaphoreType.DMA((3, n_sec)),
            pltpu.SemaphoreType.DMA,
            pltpu.SemaphoreType.DMA((7,)),
        ],
        compiler_params=pltpu.CompilerParams(
            collective_id=0, has_side_effects=True, vmem_limit_bytes=60 * 1024 * 1024
        ),
        name="section_block",
    )(
        drift_offsets.T,
        section_image,
        jnp.transpose(stem_weight, (2, 3, 1, 0)),
        jnp.transpose(first_weight, (2, 3, 4, 0, 1)),
        jnp.transpose(second_weight, (2, 3, 4, 0, 1)),
        stem_bias[None],
        first_bias[None],
        second_bias[None],
    )


def solution(mesh):
    placed = (P("sec", "row", None), P(), P(), P(), P(), P(), P(), P())
    return jax.shard_map(
        functools.partial(on_device, mesh.shape["sec"], mesh.shape["row"]),
        mesh=mesh,
        in_specs=placed,
        out_specs=P(None, None, "row", "sec"),
        check_vma=False,
    )
```

```python
import functools

import jax
import jax.numpy as jnp
from jax import lax
from jax.experimental import pallas as pl
from jax.experimental.pallas import tpu as pltpu
from jax.sharding import PartitionSpec as P

CP = 32
KJ = 256
MESH = pl.DeviceIdType.MESH


def toeplitz(base, reps, step, out_ref):
    for r in range(reps):
        out_ref[r * CP : (r + 1) * CP, :] = (
            pltpu.roll(base, step * r, 1) if r else base
        ).astype(jnp.bfloat16)


def kernel(
    n_sec, n_row, drift_ref, img_hbm, stem_hbm, w1_hbm, w2_hbm, sb_hbm, fb_hbm, cb_hbm, out_ref,
    img_ref, stem_ref, w1_ref, w2_ref, bias_rows, bias_ref,
    msg, g_ref, base, ts, t1, t2, x1, x2, send_sem, recv_sem, own_sem, in_sem,
):
    sec, row = lax.axis_index("sec"), lax.axis_index("row")
    _, rows, width = img_ref.shape
    out_width = width // 2
    n_rows, n_cols = n_row * rows // 2, out_width
    cols = out_width // n_sec
    has = {-1: row > 0, 0: None, 1: row < n_row - 1}

    def partners(act):
        for k in range(n_sec):
            for d in (-1, 1, 0):
                if d:
                    pl.when(has[d])(functools.partial(act, d, k))
                elif k:
                    act(d, k)

    loads = [
        pltpu.make_async_copy(source, target, in_sem.at[i])
        for i, (source, target) in enumerate(
            (
                (img_hbm, img_ref),
                (stem_hbm, stem_ref),
                (sb_hbm, bias_rows.at[0]),
                (fb_hbm, bias_rows.at[1]),
                (cb_hbm, bias_rows.at[2]),
                (w1_hbm, w1_ref),
                (w2_hbm, w2_ref),
            )
        )
    ]
    for load in loads:
        load.start()
    barrier = pltpu.get_barrier_semaphore()

    def greet(d, k):
        pl.semaphore_signal(
            barrier,
            inc=1,
            device_id=(lax.rem(sec + k, n_sec), row + d),
            device_id_type=MESH,
        )

    partners(greet)

    loads[0].wait()
    image = img_ref[0]
    high = image.astype(jnp.bfloat16)
    low = (image - high.astype(jnp.float32)).astype(jnp.bfloat16)
    chunks = width // 256
    stacked = jnp.concatenate(
        [part[:, c * 256 : (c + 1) * 256] for part in (high, low) for c in range(chunks)], axis=0
    )
    source = lax.broadcasted_iota(jnp.int32, (256, 256), 0)
    target = lax.broadcasted_iota(jnp.int32, (256, 256), 1)
    wanted = jnp.where(target < 128, 2 * target, 2 * target - 255)
    pick = jnp.where(source == wanted, 1.0, 0.0).astype(jnp.bfloat16)
    split = jnp.dot(stacked, pick, preferred_element_type=jnp.float32)

    def piece(part, odd, c):
        if c < 0 or c >= chunks:
            return jnp.zeros((rows, 128), jnp.float32)
        at = (part * chunks + c) * rows
        return split[at : at + rows, odd * 128 : odd * 128 + 128]

    lane = lax.broadcasted_iota(jnp.int32, (rows, 128), 1)
    per = cols // 128
    for q in range(n_sec):
        edge = jnp.zeros((rows, 128), jnp.float32)
        for part in range(2):
            for odd in range(2):
                p = 2 * part + odd
                for c in range(per):
                    at = p * cols + c * 128
                    msg[q, :, at : at + 128] = piece(part, odd, q * per + c).astype(
                        jnp.bfloat16
                    )
                left, right = piece(part, odd, q * per - 1), piece(part, odd, (q + 1) * per)
                both = jnp.where(lane >= 120, left, jnp.where(lane < 8, right, 0.0))
                edge = edge + pltpu.roll(both, p * 16 + 8, 1)
        msg[q, :, 4 * cols : 4 * cols + 128] = edge.astype(jnp.bfloat16)

    @pl.when(row == 0)
    def _():
        g_ref[0] = jnp.zeros(g_ref.shape[1:], jnp.bfloat16)

    @pl.when(row == n_row - 1)
    def _():
        g_ref[2] = jnp.zeros(g_ref.shape[1:], jnp.bfloat16)

    up = jnp.where(row > 0, 1, 0)
    down = jnp.where(row < n_row - 1, 1, 0)
    pl.semaphore_wait(barrier, n_sec * (1 + up + down) - 1)

    def outgoing(d, k):
        owner = lax.rem(sec + k, n_sec)
        return pltpu.make_async_remote_copy(
            src_ref=msg.at[owner],
            dst_ref=g_ref.at[1 - d, sec],
            send_sem=send_sem.at[1 - d, k],
            recv_sem=recv_sem.at[1 - d, k],
            device_id=(owner, row + d),
            device_id_type=MESH,
        )

    def incoming(d, k):
        origin = lax.rem(sec + n_sec - k, n_sec)
        return pltpu.make_async_remote_copy(
            src_ref=msg.at[sec],
            dst_ref=g_ref.at[1 + d, origin],
            send_sem=send_sem.at[1 + d, k],
            recv_sem=recv_sem.at[1 + d, k],
            device_id=(origin, row + d),
            device_id_type=MESH,
        )

    partners(lambda d, k: outgoing(d, k).start())
    own = pltpu.make_async_copy(msg.at[sec], g_ref.at[1, sec], own_sem)
    own.start()

    _, sections, in_rows, _ = g_ref.shape
    wide = cols + 256
    channels, _, out_rows, _ = out_ref.shape
    lanes = cols + 128
    rows_a, rows_h = out_rows + 4, out_rows + 2
    seg1, seg2 = rows_a * CP, rows_h * CP
    high_rows = 3 * in_rows

    for load in loads[1:]:
        load.wait()
    parts = [stem_ref[i, j] for i in range(5) for j in range(5)] + [bias_rows[b] for b in range(3)]
    parts.append(jnp.zeros((4, channels), jnp.float32))
    small = jnp.concatenate(parts, axis=0)
    item = lax.broadcasted_iota(jnp.int32, (32, KJ + 384), 0)
    place = lax.broadcasted_iota(jnp.int32, (32, KJ + 384), 1)
    tap_i, tap_j = item // 5, item % 5
    spot = tap_j * high_rows + in_rows - 6 + tap_i
    hit = ((item < 25) & (place < KJ) & (place == spot)) | (
        (item >= 25) & (place >= KJ) & ((place - KJ) // 128 == item - 25)
    )
    laid = lax.dot_general(
        small,
        jnp.where(hit, 1.0, 0.0),
        (((0,), (0,)), ((), ())),
        precision=lax.Precision.HIGHEST,
        preferred_element_type=jnp.float32,
    )
    laid = jnp.concatenate([laid, jnp.zeros((CP - channels, KJ + 384), jnp.float32)], axis=0)
    stem = laid[:, :KJ]
    for b in range(3):
        bias_ref[b] = laid[:, KJ + b * 128 : KJ + (b + 1) * 128]
    for r in range(rows_a):
        rolled = pltpu.roll(stem, 2 * r, 1) if r else stem
        high = rolled.astype(jnp.bfloat16)
        low = (rolled - high.astype(jnp.float32)).astype(jnp.bfloat16)
        at = slice(r * CP, (r + 1) * CP)
        ts[at, 0:KJ] = high
        ts[at, KJ : 2 * KJ] = high
        ts[at, 2 * KJ : 3 * KJ] = low
    for w_ref, seg, reps, ref in ((w1_ref, seg1, rows_h, t1), (w2_ref, seg2, out_rows, t2)):
        base[...] = jnp.zeros(base.shape, jnp.float32)
        for ds in range(3):
            for tap in range(3):
                for dx in range(3):
                    at = (ds * 3 + dx) * seg + tap * CP
                    base[0:channels, at : at + channels] = w_ref[ds, tap, dx].astype(jnp.float32)
        toeplitz(base[:, : ref.shape[1]], reps, CP, ref)
    nothing = jnp.zeros((3 * seg1, lanes), jnp.bfloat16)
    x1[0 : 3 * seg1, :] = nothing
    x1[(sections + 1) * 3 * seg1 :, :] = nothing
    x2[0 : 3 * seg2, :] = nothing[: 3 * seg2]
    tail = x2.shape[0] - (sections + 1) * 3 * seg2
    x2[(sections + 1) * 3 * seg2 :, :] = nothing[:tail]

    def inside(first, size, limit, axis, repeat, shift=None):
        shape = (size * repeat, 1) if axis == 0 else (1, size)
        pos = lax.broadcasted_iota(jnp.int32, shape, axis)
        pos = (pos // repeat if repeat > 1 else pos) + first
        ok = (pos >= 0) & (pos < limit)
        if shift is not None:
            ok = ok & (pos + shift >= 0) & (pos + shift < limit)
        return jnp.where(ok, 1.0, 0.0)

    def column(which, reps):
        return jnp.concatenate([bias_ref[which, :, 0:1]] * reps, axis=0)

    def spread(value, ref, start, seg):
        for d in range(3):
            moved = pltpu.roll(value, lanes - d, 1) if d else value
            ref[pl.ds(pl.multiple_of(start + d * seg, CP), seg), :] = moved.astype(jnp.bfloat16)

    own.wait()
    first_row, first_col = row * out_rows, sec * cols

    def stem_step(k, carry):
        s = lax.rem(sec + n_sec - k, n_sec)
        for d, there in ((-1, has[-1]), (1, has[1]), (0, k > 0)):
            pl.when(there)(lambda d=d: incoming(d, k).wait_recv())
        dr, dc = drift_ref[0, s], drift_ref[1, s]
        taps = []
        for odd in range(2):
            blocks = []
            for b in range(3):
                rim = g_ref[b, s, :, 4 * cols : 4 * cols + 128].astype(jnp.float32)
                total = None
                for p in (odd, 2 + odd):
                    ends = pltpu.roll(rim, 120 - 16 * p, 1)
                    main = g_ref[b, s, :, p * cols : (p + 1) * cols].astype(jnp.float32)
                    part = jnp.concatenate([ends, main, ends], axis=1)
                    total = part if total is None else total + part
                blocks.append(total)
            plane = jnp.concatenate(blocks, axis=0)
            plane = pltpu.roll(plane, lax.rem(high_rows - 2 * dr, high_rows), 0)
            taps.append(pltpu.roll(plane, wide - 126 - dc, 1))
        even, odd = taps
        shifted = [
            pltpu.roll(even, 1, 1),
            pltpu.roll(odd, 1, 1),
            even,
            odd,
            pltpu.roll(even, wide - 1, 1),
        ]
        field = jnp.concatenate(
            [part[:, :lanes] for part in shifted]
            + [jnp.zeros((KJ - 5 * high_rows, lanes), jnp.float32)],
            axis=0,
        )
        high = field.astype(jnp.bfloat16)
        low = (field - high.astype(jnp.float32)).astype(jnp.bfloat16)
        result = jnp.dot(
            ts[...], jnp.concatenate([high, low, high], axis=0), preferred_element_type=jnp.float32
        )
        result = jnp.maximum(result + column(0, rows_a), 0.0)
        result = result * inside(first_row - 2, rows_a, n_rows, 0, CP, dr)
        result = result * inside(first_col - 2, lanes, n_cols, 1, 1, dc)
        spread(result, x1, (s + 1) * 3 * seg1, seg1)
        return carry

    lax.fori_loop(0, sections, stem_step, 0)

    def first_step(s, carry):
        at = pl.ds(pl.multiple_of(s * 3 * seg1, CP), t1.shape[1])
        result = jnp.dot(t1[...], x1[at, :], preferred_element_type=jnp.float32)
        result = jnp.maximum(result + column(1, rows_h), 0.0)
        result = result * inside(first_row - 1, rows_h, n_rows, 0, CP)
        result = result * inside(first_col - 1, lanes, n_cols, 1, 1)
        spread(result, x2, (s + 1) * 3 * seg2, seg2)
        return carry

    lax.fori_loop(0, sections, first_step, 0)

    def second_step(s, carry):
        at = pl.ds(pl.multiple_of(s * 3 * seg2, CP), t2.shape[1])
        result = jnp.dot(t2[...], x2[at, 0:cols], preferred_element_type=jnp.float32)
        start = (s + 1) * 3 * seg1 + 2 * seg1 + 2 * CP
        kept = x1[pl.ds(pl.multiple_of(start, CP), out_rows * CP), 0:cols]
        result = result + column(2, out_rows) + kept.astype(jnp.float32)
        result = jnp.swapaxes(result.reshape(out_rows, CP, cols), 0, 1)
        out_ref[:, pl.ds(s, 1)] = result[:channels, None].astype(jnp.bfloat16)
        return carry

    lax.fori_loop(0, sections, second_step, 0)
    partners(lambda d, k: outgoing(d, k).wait_send())


def on_device(
    n_sec,
    n_row,
    section_image,
    drift_offsets,
    stem_weight,
    stem_bias,
    first_weight,
    first_bias,
    second_weight,
    second_bias,
):
    _, in_rows, width = section_image.shape
    sections = n_sec
    channels = stem_weight.shape[0]
    out_rows, out_width = in_rows // 2, width // 2
    cols = out_width // n_sec
    lanes = cols + 128
    vmem = pl.BlockSpec(memory_space=pltpu.VMEM)
    k1 = 9 * (out_rows + 4) * CP
    k2 = -(-9 * (out_rows + 2) * CP // 128) * 128
    seg1, seg2 = (out_rows + 4) * CP, (out_rows + 2) * CP
    return pl.pallas_call(
        functools.partial(kernel, n_sec, n_row),
        out_shape=pltpu.VMEM((channels, sections, out_rows, cols), jnp.bfloat16),
        in_specs=[pl.BlockSpec(memory_space=pltpu.SMEM)] + [pl.BlockSpec(memory_space=pltpu.HBM)] * 7,
        out_specs=vmem,
        scratch_shapes=[
            pltpu.VMEM(section_image.shape, jnp.float32),
            pltpu.VMEM((5, 5, 1, channels), jnp.float32),
            pltpu.VMEM((3, 3, 3, channels, channels), jnp.bfloat16),
            pltpu.VMEM((3, 3, 3, channels, channels), jnp.bfloat16),
            pltpu.VMEM((3, 1, channels), jnp.float32),
            pltpu.VMEM((3, CP, 128), jnp.float32),
            pltpu.VMEM((n_sec, in_rows, 4 * cols + 128), jnp.bfloat16),
            pltpu.VMEM((3, sections, in_rows, 4 * cols + 128), jnp.bfloat16),
            pltpu.VMEM((CP, max(k1, k2)), jnp.float32),
            pltpu.VMEM((seg1, 3 * KJ), jnp.bfloat16),
            pltpu.VMEM((seg2, k1), jnp.bfloat16),
            pltpu.VMEM((out_rows * CP, k2), jnp.bfloat16),
            pltpu.VMEM(((sections + 2) * 3 * seg1, lanes), jnp.bfloat16),
            pltpu.VMEM(((sections + 2) * 3 * seg2 + k2 - 9 * seg2, lanes), jnp.bfloat16),
            pltpu.SemaphoreType.DMA((3, n_sec)),
            pltpu.SemaphoreType.DMA((3, n_sec)),
            pltpu.SemaphoreType.DMA,
            pltpu.SemaphoreType.DMA((7,)),
        ],
        compiler_params=pltpu.CompilerParams(
            collective_id=0, has_side_effects=True, vmem_limit_bytes=60 * 1024 * 1024
        ),
        name="section_block",
    )(
        drift_offsets.T,
        section_image,
        jnp.transpose(stem_weight, (2, 3, 1, 0)),
        jnp.transpose(first_weight, (2, 3, 4, 0, 1)),
        jnp.transpose(second_weight, (2, 3, 4, 0, 1)),
        stem_bias[None],
        first_bias[None],
        second_bias[None],
    )


def solution(mesh):
    placed = (P("sec", "row", None), P(), P(), P(), P(), P(), P(), P())
    return jax.shard_map(
        functools.partial(on_device, mesh.shape["sec"], mesh.shape["row"]),
        mesh=mesh,
        in_specs=placed,
        out_specs=P(None, None, "row", "sec"),
        check_vma=False,
    )
```
